32 devices in a mesh: tgt: 8 (over z, y), src: 4 (over x, core).
Axes of the slice: x: 2, y: 2, z: 4, core: 2. Of those that a mesh axis runs over, the one named last changes fastest.
Arguments:
- coefficients: bfloat16 [32, 4, 512, 512], P('tgt', 'src'), may hold values from -1.5 to 1.5
- factors: bfloat16 [3, 32, 4, 512, 512], P(None, 'tgt', 'src'), may hold values from -0.25 to 0.25
Outputs:
- potentials: float32 [32, 2, 256, 512], P('tgt', None, 'src')
The draws below stay inside these ranges and needn't reach their ends.
All inputs are finite; a program needn't handle non-finite values.
Results may differ from the reference program's by a relative error of at most 0.013.
Values may be sent and summed in bfloat16 or wider, within the bound.
A program may use at most 64 MiB of HBM per device.

```python
import jax
import jax.numpy as jnp
from jax import lax

R = 256
RHS = 512
BLK = 4
LEVELS = 3
TBLOCKS = 32
N_TGT = 8
N_SRC = 4


def levels(own_key, extent, cuts, low, top_value):
    level, own = 1.0, jax.random.fold_in(own_key, 6)
    for dim, blocks in cuts:
        steps = jnp.exp(jax.random.uniform(jax.random.fold_in(own, dim), (blocks,), jnp.float32, low / len(cuts), top_value / len(cuts)))
        level = level * jnp.repeat(steps, extent[dim] // blocks).reshape([-1 if axis == dim else 1 for axis in range(len(extent))])
    return level


def centred(key, extent, spread, reach, pieces=(), kind=jnp.bfloat16):
    loudness = levels(key, extent, pieces, -0.22, 0.18) if pieces else 1.0
    result = jax.random.normal(key, extent, jnp.float32) * spread * loudness
    return jnp.minimum(jnp.maximum(result, -reach), reach).astype(kind)


def setup_inputs(seed: int = 0) -> dict:
    splits = jax.random.split(jax.random.key(seed), 3)
    return {
        "coefficients": centred(splits[0], (TBLOCKS, N_SRC, 2 * R, RHS), 0.25, 1.5, ((0, 8), (1, 4))),
        "factors": centred(splits[1], (LEVELS, TBLOCKS, N_SRC, 2 * R, 2 * R), (2 * R) ** -0.5, 0.25, ((1, 8), (2, 4))),
    }


def reference(coefficients, factors):
    total_blocks = coefficients.shape[0]
    bit_count = N_TGT.bit_length() - 1
    current = coefficients
    for section_index in range(LEVELS):
        def mix_block(block_index):
            weights = factors[section_index, block_index].astype(jnp.float32)
            block = current[block_index].astype(jnp.float32)
            return jnp.einsum('sij,sjn->sin', weights, block).astype(jnp.bfloat16)

        blended = lax.map(mix_block, jnp.arange(total_blocks, dtype=jnp.int32))
        shift = section_index % bit_count
        partner = jnp.bitwise_xor(jnp.arange(total_blocks, dtype=jnp.int32), jnp.int32(BLK << shift))
        lower = jnp.take(blended[:, :, R:], partner, axis=0)
        current = jnp.concatenate([blended[:, :, :R], lower], axis=2)
    summed = jnp.sum(current.astype(jnp.float32), axis=1)
    return summed.reshape(total_blocks, 2, R, summed.shape[-1])
```

```python
import functools

import jax
import jax.numpy as jnp
from jax import lax
from jax.experimental import pallas as pl
from jax.experimental.pallas import tpu as pltpu
from jax.sharding import PartitionSpec as P

PARTS = 4
READY = 1
LAGS = (3, 7)
HOLD = 6


def kernel(sizes, coef_ref, fact_ref, out_ref, *scratch):
    n_tgt, n_src, levels, blocks, half, width, parts, lags, ready, hold = sizes
    chunks, rows = blocks * parts, half // n_src
    coef, fact, current, sends, part, inbox, low_send, low_recv = scratch[:8]
    first_sem, load_sem, lev_send, lev_recv, src_send, src_recv, low_sent, low_got = scratch[8:]
    me = lax.axis_index("tgt")
    src = lax.axis_index("src")
    bits = n_tgt.bit_length() - 1

    def partner(level):
        step = 1 << level % bits
        return me + step * (1 - 2 * ((me // step) % 2))

    def peer(k):
        return (src + k) % n_src

    def load_first(b):
        return (
            pltpu.make_async_copy(coef_ref.at[b], coef.at[b], first_sem.at[0, b]),
            pltpu.make_async_copy(fact_ref.at[0, b], fact.at[0, b], first_sem.at[1, b]),
        )

    def load(level):
        return pltpu.make_async_copy(fact_ref.at[level], fact.at[level], load_sem.at[level - 1])

    barrier = pltpu.get_barrier_semaphore()
    shifts = sorted({level % bits for level in range(levels)})
    for shift in shifts:
        pl.semaphore_signal(
            barrier, inc=1, device_id={"tgt": partner(shift)}, device_id_type=pl.DeviceIdType.MESH
        )
    for k in range(1, n_src):
        pl.semaphore_signal(
            barrier, inc=1, device_id={"src": peer(k)}, device_id_type=pl.DeviceIdType.MESH
        )

    for b in range(blocks):
        for copy in load_first(b):
            copy.start()
    for level in range(1, levels):
        load(level).start()

    def exchange(level, c):
        return pltpu.make_async_remote_copy(
            src_ref=sends.at[level, c],
            dst_ref=current.at[level, c, pl.ds(half, half)],
            send_sem=lev_send.at[0],
            recv_sem=lev_recv.at[level, c],
            device_id={"tgt": partner(level)},
            device_id_type=pl.DeviceIdType.MESH,
        )

    def scatter(k, c):
        return pltpu.make_async_remote_copy(
            src_ref=part.at[c, peer(k)],
            dst_ref=inbox.at[c, k - 1],
            send_sem=src_send.at[0],
            recv_sem=src_recv.at[c],
            device_id={"src": peer(k)},
            device_id_type=pl.DeviceIdType.MESH,
        )

    def lower(c):
        return pltpu.make_async_remote_copy(
            src_ref=low_send.at[c],
            dst_ref=low_recv.at[c],
            send_sem=low_sent.at[0],
            recv_sem=low_got.at[c // parts],
            device_id={"tgt": partner(levels - 1)},
            device_id_type=pl.DeviceIdType.MESH,
        )

    def whole(ref, sem):
        return pltpu.make_async_copy(ref, ref, sem)

    def columns(c):
        return pl.ds(pl.multiple_of((c % parts) * width, width), width)

    def write(side, c, value):
        out_ref[c // parts, side, :, columns(c)] = value

    def blend(level, c, rows):
        value = current[level - 1, c] if level else coef[c // parts, :, columns(c)]
        return jnp.dot(
            fact[level, c // parts, rows], value, preferred_element_type=jnp.float32
        ).astype(jnp.bfloat16)

    upper_rows, lower_rows = pl.ds(0, half), pl.ds(half, half)

    def wait_factor(level, c):
        @pl.when(c == 0)
        def _():
            load(level).wait()

    def prepare(c, carry):
        @pl.when(c % parts == 0)
        def _():
            for copy in load_first(c // parts):
                copy.wait()

        sends[0, c] = blend(0, c, lower_rows)
        return carry

    def send_first(c, carry):
        exchange(0, c).start()
        return carry

    def prepare_send(c, carry):
        prepare(c, carry)
        return send_first(c, carry)

    def middle(level, c):
        current[level - 1, c, :half] = blend(level - 1, c, upper_rows)
        wait_factor(level, c)
        exchange(level - 1, c).wait_recv()
        sends[level, c] = blend(level, c, lower_rows)
        exchange(level, c).start()

    def final(c):
        level = levels - 1
        current[level - 1, c, :half] = blend(level - 1, c, upper_rows)
        wait_factor(level, c)
        exchange(level - 1, c).wait_recv()
        blended = blend(level, c, pl.ds(0, 2 * half))
        for j in range(n_src):
            part[c, j, 0] = blended[j * rows : (j + 1) * rows]
            part[c, j, 1] = blended[half + j * rows : half + (j + 1) * rows]
        for k in range(1, n_src):
            scatter(k, c).start()

    def sum_stage(c):
        total = part[c, src].astype(jnp.float32)
        whole(inbox.at[c], src_recv.at[c]).wait()
        for k in range(1, n_src):
            total += inbox[c, k - 1].astype(jnp.float32)
        low_send[c] = total[1].astype(jnp.bfloat16)
        write(0, c, total[0])

    lax.fori_loop(0, ready, prepare, 0)
    pl.semaphore_wait(barrier, len(shifts) + n_src - 1)
    lax.fori_loop(0, ready, send_first, 0)
    lax.fori_loop(ready, chunks, prepare_send, 0)

    def sum_and_send(i, c):
        sum_stage(c)

        @pl.when(jnp.logical_or(c < hold, i >= chunks - 1))
        def _():
            lower(c).start()

    def release(c, carry):
        lower(c).start()
        return carry

    stages = [functools.partial(middle, level) for level in range(1, levels - 1)] + [final]
    lag_sum = lags[-1]

    def step(i, carry):
        for stage, lag in zip(stages, (0,) + lags):
            c = i - lag

            @pl.when(jnp.logical_and(c >= 0, c < chunks))
            def _():
                stage(c)

        @pl.when(i == chunks - 1)
        def _():
            lax.fori_loop(hold, max(hold, chunks - 1 - lag_sum), release, 0)

        c = i - lag_sum

        @pl.when(jnp.logical_and(c >= 0, c < chunks))
        def _():
            sum_and_send(i, c)

        return carry

    lax.fori_loop(0, chunks + lag_sum, step, 0)

    whole(sends, lev_send.at[0]).wait()
    whole(inbox, src_send.at[0]).wait()
    whole(low_send, low_sent.at[0]).wait()

    def last_stage(b, carry):
        group = pl.ds(b * parts, parts)
        whole(low_recv.at[group], low_got.at[b]).wait()
        for h in range(parts):
            out_ref[b, 1, :, h * width : (h + 1) * width] = low_recv[b * parts + h].astype(jnp.float32)
        return carry

    lax.fori_loop(0, blocks, last_stage, 0)


def local(n_tgt, n_src, coefficients, factors):
    levels, blocks = factors.shape[0], factors.shape[1]
    size, columns = coefficients.shape[2], coefficients.shape[3]
    half, width = size // 2, columns // PARTS
    chunks, rows = blocks * PARTS, half // n_src
    dma = pltpu.SemaphoreType.DMA
    bf16 = jnp.bfloat16
    return pl.pallas_call(
        functools.partial(
            kernel,
            (n_tgt, n_src, levels, blocks, half, width, PARTS, LAGS, min(READY, chunks), min(HOLD, chunks)),
        ),
        out_shape=pltpu.VMEM((blocks, 2, rows, columns), jnp.float32),
        in_specs=[pl.BlockSpec(memory_space=pl.ANY)] * 2,
        out_specs=pl.BlockSpec(memory_space=pltpu.VMEM),
        scratch_shapes=[
            pltpu.VMEM((blocks, size, columns), bf16),
            pltpu.VMEM((levels, blocks, size, size), bf16),
            pltpu.VMEM((levels - 1, chunks, size, width), bf16),
            pltpu.VMEM((levels - 1, chunks, half, width), bf16),
            pltpu.VMEM((chunks, n_src, 2, rows, width), bf16),
            pltpu.VMEM((chunks, n_src - 1, 2, rows, width), bf16),
            pltpu.VMEM((chunks, rows, width), bf16),
            pltpu.VMEM((chunks, rows, width), bf16),
            dma((2, blocks)),
            dma((levels - 1,)),
            dma((1,)),
            dma((levels - 1, chunks)),
            dma((1,)),
            dma((chunks,)),
            dma((1,)),
            dma((blocks,)),
        ],
        compiler_params=pltpu.CompilerParams(collective_id=0, has_side_effects=True),
    )(coefficients[:, 0], factors[:, :, 0])


def solution(mesh):
    placed = (P("tgt", "src", None, None), P(None, "tgt", "src", None, None))
    return jax.shard_map(
        functools.partial(local, mesh.shape["tgt"], mesh.shape["src"]),
        mesh=mesh,
        in_specs=placed,
        out_specs=P("tgt", None, "src", None),
        check_vma=False,
    )
```

```python
import functools

import jax
import jax.numpy as jnp
from jax import lax
from jax.experimental import pallas as pl
from jax.experimental.pallas import tpu as pltpu
from jax.sharding import PartitionSpec as P

PARTS = 4
READY = 1
LAGS = (3, 8)
HOLD = 6


def kernel(sizes, coef_ref, fact_ref, out_ref, *scratch):
    n_tgt, n_src, levels, blocks, half, width, parts, lags, ready, hold = sizes
    chunks, rows = blocks * parts, half // n_src
    coef, fact, current, sends, part, inbox, low_send, low_recv = scratch[:8]
    first_sem, load_sem, lev_send, lev_recv, src_send, src_recv, low_sent, low_got = scratch[8:]
    me = lax.axis_index("tgt")
    src = lax.axis_index("src")
    bits = n_tgt.bit_length() - 1

    def partner(level):
        step = 1 << level % bits
        return me + step * (1 - 2 * ((me // step) % 2))

    def peer(k):
        return (src + k) % n_src

    def load_first(b):
        return (
            pltpu.make_async_copy(coef_ref.at[b], coef.at[b], first_sem.at[0, b]),
            pltpu.make_async_copy(fact_ref.at[0, b], fact.at[0, b], first_sem.at[1, b]),
        )

    def load(level):
        return pltpu.make_async_copy(fact_ref.at[level], fact.at[level], load_sem.at[level - 1])

    barrier = pltpu.get_barrier_semaphore()
    shifts = sorted({level % bits for level in range(levels)})
    for shift in shifts:
        pl.semaphore_signal(
            barrier, inc=1, device_id={"tgt": partner(shift)}, device_id_type=pl.DeviceIdType.MESH
        )
    for k in range(1, n_src):
        pl.semaphore_signal(
            barrier, inc=1, device_id={"src": peer(k)}, device_id_type=pl.DeviceIdType.MESH
        )

    for b in range(blocks):
        for copy in load_first(b):
            copy.start()
    for level in range(1, levels):
        load(level).start()

    def exchange(level, c):
        return pltpu.make_async_remote_copy(
            src_ref=sends.at[level, c],
            dst_ref=current.at[level, c, pl.ds(half, half)],
            send_sem=lev_send.at[0],
            recv_sem=lev_recv.at[level, c],
            device_id={"tgt": partner(level)},
            device_id_type=pl.DeviceIdType.MESH,
        )

    def scatter(k, c):
        return pltpu.make_async_remote_copy(
            src_ref=part.at[c, peer(k)],
            dst_ref=inbox.at[c, k - 1],
            send_sem=src_send.at[0],
            recv_sem=src_recv.at[c],
            device_id={"src": peer(k)},
            device_id_type=pl.DeviceIdType.MESH,
        )

    def lower(c):
        return pltpu.make_async_remote_copy(
            src_ref=low_send.at[c],
            dst_ref=low_recv.at[c],
            send_sem=low_sent.at[0],
            recv_sem=low_got.at[c // parts],
            device_id={"tgt": partner(levels - 1)},
            device_id_type=pl.DeviceIdType.MESH,
        )

    def whole(ref, sem):
        return pltpu.make_async_copy(ref, ref, sem)

    def columns(c):
        return pl.ds(pl.multiple_of((c % parts) * width, width), width)

    def write(side, c, value):
        out_ref[c // parts, side, :, columns(c)] = value

    def blend(level, c, rows):
        value = current[level - 1, c] if level else coef[c // parts, :, columns(c)]
        return jnp.dot(
            fact[level, c // parts, rows], value, preferred_element_type=jnp.float32
        ).astype(jnp.bfloat16)

    upper_rows, lower_rows = pl.ds(0, half), pl.ds(half, half)

    def wait_factor(level, c):
        @pl.when(c == 0)
        def _():
            load(level).wait()

    def prepare(c, carry):
        @pl.when(c % parts == 0)
        def _():
            for copy in load_first(c // parts):
                copy.wait()

        sends[0, c] = blend(0, c, lower_rows)
        return carry

    def send_first(c, carry):
        exchange(0, c).start()
        return carry

    def prepare_send(c, carry):
        prepare(c, carry)
        return send_first(c, carry)

    def middle(level, c):
        current[level - 1, c, :half] = blend(level - 1, c, upper_rows)
        wait_factor(level, c)
        exchange(level - 1, c).wait_recv()
        sends[level, c] = blend(level, c, lower_rows)
        exchange(level, c).start()

    def final(c):
        level = levels - 1
        current[level - 1, c, :half] = blend(level - 1, c, upper_rows)
        wait_factor(level, c)
        exchange(level - 1, c).wait_recv()
        blended = blend(level, c, pl.ds(0, 2 * half))
        for j in range(n_src):
            part[c, j, 0] = blended[j * rows : (j + 1) * rows]
            part[c, j, 1] = blended[half + j * rows : half + (j + 1) * rows]
        for k in range(1, n_src):
            scatter(k, c).start()

    def sum_stage(c):
        total = part[c, src].astype(jnp.float32)
        whole(inbox.at[c], src_recv.at[c]).wait()
        for k in range(1, n_src):
            total += inbox[c, k - 1].astype(jnp.float32)
        low_send[c] = total[1].astype(jnp.bfloat16)
        write(0, c, total[0])

    lax.fori_loop(0, ready, prepare, 0)
    pl.semaphore_wait(barrier, len(shifts) + n_src - 1)
    lax.fori_loop(0, ready, send_first, 0)
    lax.fori_loop(ready, chunks, prepare_send, 0)

    near, far = 1 << (levels - 2) % bits, 1 << (levels - 1) % bits
    inner = (me // near) % 2 != (me // far) % 2
    held = jnp.where(inner, 16, 0)

    def sum_and_send(i, c):
        sum_stage(c)

        @pl.when(jnp.logical_or(c < held, i >= chunks - 1))
        def _():
            lower(c).start()

    def release(c, carry):
        lower(c).start()
        return carry

    stages = [functools.partial(middle, level) for level in range(1, levels - 1)] + [final]
    lag_sum = lags[-1]

    def step(i, carry):
        for stage, lag in zip(stages, (0,) + lags):
            c = i - lag

            @pl.when(jnp.logical_and(c >= 0, c < chunks))
            def _():
                stage(c)

        @pl.when(i == chunks - 1)
        def _():
            lax.fori_loop(held, jnp.maximum(held, chunks - 1 - lag_sum), release, 0)

        c = i - lag_sum

        @pl.when(jnp.logical_and(c >= 0, c < chunks))
        def _():
            sum_and_send(i, c)

        return carry

    lax.fori_loop(0, chunks + lag_sum, step, 0)

    whole(sends, lev_send.at[0]).wait()
    whole(inbox, src_send.at[0]).wait()
    whole(low_send, low_sent.at[0]).wait()

    def last_stage(b, carry):
        group = pl.ds(b * parts, parts)
        whole(low_recv.at[group], low_got.at[b]).wait()
        for h in range(parts):
            out_ref[b, 1, :, h * width : (h + 1) * width] = low_recv[b * parts + h].astype(jnp.float32)
        return carry

    lax.fori_loop(0, blocks, last_stage, 0)


def local(n_tgt, n_src, coefficients, factors):
    levels, blocks = factors.shape[0], factors.shape[1]
    size, columns = coefficients.shape[2], coefficients.shape[3]
    half, width = size // 2, columns // PARTS
    chunks, rows = blocks * PARTS, half // n_src
    dma = pltpu.SemaphoreType.DMA
    bf16 = jnp.bfloat16
    return pl.pallas_call(
        functools.partial(
            kernel,
            (n_tgt, n_src, levels, blocks, half, width, PARTS, LAGS, min(READY, chunks), min(HOLD, chunks)),
        ),
        out_shape=pltpu.VMEM((blocks, 2, rows, columns), jnp.float32),
        in_specs=[pl.BlockSpec(memory_space=pl.ANY)] * 2,
        out_specs=pl.BlockSpec(memory_space=pltpu.VMEM),
        scratch_shapes=[
            pltpu.VMEM((blocks, size, columns), bf16),
            pltpu.VMEM((levels, blocks, size, size), bf16),
            pltpu.VMEM((levels - 1, chunks, size, width), bf16),
            pltpu.VMEM((levels - 1, chunks, half, width), bf16),
            pltpu.VMEM((chunks, n_src, 2, rows, width), bf16),
            pltpu.VMEM((chunks, n_src - 1, 2, rows, width), bf16),
            pltpu.VMEM((chunks, rows, width), bf16),
            pltpu.VMEM((chunks, rows, width), bf16),
            dma((2, blocks)),
            dma((levels - 1,)),
            dma((1,)),
            dma((levels - 1, chunks)),
            dma((1,)),
            dma((chunks,)),
            dma((1,)),
            dma((blocks,)),
        ],
        compiler_params=pltpu.CompilerParams(collective_id=0, has_side_effects=True),
    )(coefficients[:, 0], factors[:, :, 0])


def solution(mesh):
    placed = (P("tgt", "src", None, None), P(None, "tgt", "src", None, None))
    return jax.shard_map(
        functools.partial(local, mesh.shape["tgt"], mesh.shape["src"]),
        mesh=mesh,
        in_specs=placed,
        out_specs=P("tgt", None, "src", None),
        check_vma=False,
    )
```

```python
import functools

import jax
import jax.numpy as jnp
from jax import lax
from jax.experimental import pallas as pl
from jax.experimental.pallas import tpu as pltpu
from jax.sharding import PartitionSpec as P

PARTS = 4
READY = 1
LAGS = (3, 8)


def kernel(sizes, coef_ref, fact_ref, out_ref, *scratch):
    n_tgt, n_src, levels, blocks, half, width, parts, lags, ready = sizes
    chunks, rows = blocks * parts, half // n_src
    coef, fact, current, sends, part, inbox, low_send, low_recv = scratch[:8]
    first_sem, load_sem, lev_send, lev_recv, src_send, src_recv, low_sent, low_got = scratch[8:]
    me = lax.axis_index("tgt")
    src = lax.axis_index("src")
    bits = n_tgt.bit_length() - 1

    def partner(level):
        step = 1 << level % bits
        return me + step * (1 - 2 * ((me // step) % 2))

    def peer(k):
        return (src + k) % n_src

    def load_first(b):
        return (
            pltpu.make_async_copy(coef_ref.at[b], coef.at[b], first_sem.at[0, b]),
            pltpu.make_async_copy(fact_ref.at[0, b], fact.at[0, b], first_sem.at[1, b]),
        )

    def load(level):
        return pltpu.make_async_copy(fact_ref.at[level], fact.at[level], load_sem.at[level - 1])

    barrier = pltpu.get_barrier_semaphore()
    shifts = sorted({level % bits for level in range(levels)})
    for shift in shifts:
        pl.semaphore_signal(
            barrier, inc=1, device_id={"tgt": partner(shift)}, device_id_type=pl.DeviceIdType.MESH
        )
    for k in range(1, n_src):
        pl.semaphore_signal(
            barrier, inc=1, device_id={"src": peer(k)}, device_id_type=pl.DeviceIdType.MESH
        )

    for b in range(blocks):
        for copy in load_first(b):
            copy.start()
    for level in range(1, levels):
        load(level).start()

    def exchange(level, c):
        return pltpu.make_async_remote_copy(
            src_ref=sends.at[level, c],
            dst_ref=current.at[level, c, pl.ds(half, half)],
            send_sem=lev_send.at[0],
            recv_sem=lev_recv.at[level, c],
            device_id={"tgt": partner(level)},
            device_id_type=pl.DeviceIdType.MESH,
        )

    def scatter(k, c):
        return pltpu.make_async_remote_copy(
            src_ref=part.at[c, peer(k)],
            dst_ref=inbox.at[c, k - 1],
            send_sem=src_send.at[0],
            recv_sem=src_recv.at[c],
            device_id={"src": peer(k)},
            device_id_type=pl.DeviceIdType.MESH,
        )

    def lower(c):
        return pltpu.make_async_remote_copy(
            src_ref=low_send.at[c],
            dst_ref=low_recv.at[c],
            send_sem=low_sent.at[0],
            recv_sem=low_got.at[c // parts],
            device_id={"tgt": partner(levels - 1)},
            device_id_type=pl.DeviceIdType.MESH,
        )

    def whole(ref, sem):
        return pltpu.make_async_copy(ref, ref, sem)

    def columns(c):
        return pl.ds(pl.multiple_of((c % parts) * width, width), width)

    def write(side, c, value):
        out_ref[c // parts, side, :, columns(c)] = value

    def blend(level, c, rows):
        value = current[level - 1, c] if level else coef[c // parts, :, columns(c)]
        return jnp.dot(
            fact[level, c // parts, rows], value, preferred_element_type=jnp.float32
        ).astype(jnp.bfloat16)

    upper_rows, lower_rows = pl.ds(0, half), pl.ds(half, half)

    def wait_factor(level, c):
        @pl.when(c == 0)
        def _():
            load(level).wait()

    def prepare(c, carry):
        @pl.when(c % parts == 0)
        def _():
            for copy in load_first(c // parts):
                copy.wait()

        sends[0, c] = blend(0, c, lower_rows)
        return carry

    def send_first(c, carry):
        exchange(0, c).start()
        return carry

    def prepare_send(c, carry):
        prepare(c, carry)
        return send_first(c, carry)

    def middle(level, c):
        current[level - 1, c, :half] = blend(level - 1, c, upper_rows)
        wait_factor(level, c)
        exchange(level - 1, c).wait_recv()
        sends[level, c] = blend(level, c, lower_rows)
        exchange(level, c).start()

    def final(c):
        level = levels - 1
        current[level - 1, c, :half] = blend(level - 1, c, upper_rows)
        wait_factor(level, c)
        exchange(level - 1, c).wait_recv()
        blended = blend(level, c, pl.ds(0, 2 * half))
        for j in range(n_src):
            part[c, j, 0] = blended[j * rows : (j + 1) * rows]
            part[c, j, 1] = blended[half + j * rows : half + (j + 1) * rows]
        for k in range(1, n_src):
            scatter(k, c).start()

    def sum_stage(c, send):
        total = part[c, src].astype(jnp.float32)
        whole(inbox.at[c], src_recv.at[c]).wait()
        for k in range(1, n_src):
            total += inbox[c, k - 1].astype(jnp.float32)
        low_send[c] = total[1].astype(jnp.bfloat16)
        send()
        write(0, c, total[0])

    lax.fori_loop(0, ready, prepare, 0)
    pl.semaphore_wait(barrier, len(shifts) + n_src - 1)
    lax.fori_loop(0, ready, send_first, 0)
    lax.fori_loop(ready, chunks, prepare_send, 0)

    near, far = 1 << (levels - 2) % bits, 1 << (levels - 1) % bits
    inner = (me // near) % 2 != (me // far) % 2
    held = jnp.where(inner, chunks, 0)

    def sum_and_send(i, c):
        def send():
            @pl.when(jnp.logical_or(c < held, i >= chunks - 1))
            def _():
                lower(c).start()

        sum_stage(c, send)

    def release(c, carry):
        lower(c).start()
        return carry

    stages = [functools.partial(middle, level) for level in range(1, levels - 1)] + [final]
    lag_sum = lags[-1]

    def step(i, carry):
        for stage, lag in zip(stages, (0,) + lags):
            c = i - lag

            @pl.when(jnp.logical_and(c >= 0, c < chunks))
            def _():
                stage(c)

        @pl.when(i == chunks - 1)
        def _():
            lax.fori_loop(held, jnp.maximum(held, chunks - 1 - lag_sum), release, 0)

        c = i - lag_sum

        @pl.when(jnp.logical_and(c >= 0, c < chunks))
        def _():
            sum_and_send(i, c)

        return carry

    lax.fori_loop(0, chunks + lag_sum, step, 0)

    def last_stage(b, carry):
        group = pl.ds(b * parts, parts)
        whole(low_recv.at[group], low_got.at[b]).wait()
        for h in range(parts):
            out_ref[b, 1, :, h * width : (h + 1) * width] = low_recv[b * parts + h].astype(jnp.float32)
        return carry

    lax.fori_loop(0, blocks, last_stage, 0)
    whole(sends, lev_send.at[0]).wait()
    whole(inbox, src_send.at[0]).wait()
    whole(low_send, low_sent.at[0]).wait()


def local(n_tgt, n_src, coefficients, factors):
    levels, blocks = factors.shape[0], factors.shape[1]
    size, columns = coefficients.shape[2], coefficients.shape[3]
    half, width = size // 2, columns // PARTS
    chunks, rows = blocks * PARTS, half // n_src
    dma = pltpu.SemaphoreType.DMA
    bf16 = jnp.bfloat16
    return pl.pallas_call(
        functools.partial(
            kernel,
            (n_tgt, n_src, levels, blocks, half, width, PARTS, LAGS, min(READY, chunks)),
        ),
        out_shape=pltpu.VMEM((blocks, 2, rows, columns), jnp.float32),
        in_specs=[pl.BlockSpec(memory_space=pl.ANY)] * 2,
        out_specs=pl.BlockSpec(memory_space=pltpu.VMEM),
        scratch_shapes=[
            pltpu.VMEM((blocks, size, columns), bf16),
            pltpu.VMEM((levels, blocks, size, size), bf16),
            pltpu.VMEM((levels - 1, chunks, size, width), bf16),
            pltpu.VMEM((levels - 1, chunks, half, width), bf16),
            pltpu.VMEM((chunks, n_src, 2, rows, width), bf16),
            pltpu.VMEM((chunks, n_src - 1, 2, rows, width), bf16),
            pltpu.VMEM((chunks, rows, width), bf16),
            pltpu.VMEM((chunks, rows, width), bf16),
            dma((2, blocks)),
            dma((levels - 1,)),
            dma((1,)),
            dma((levels - 1, chunks)),
            dma((1,)),
            dma((chunks,)),
            dma((1,)),
            dma((blocks,)),
        ],
        compiler_params=pltpu.CompilerParams(collective_id=0, has_side_effects=True),
    )(coefficients[:, 0], factors[:, :, 0])


def solution(mesh):
    placed = (P("tgt", "src", None, None), P(None, "tgt", "src", None, None))
    return jax.shard_map(
        functools.partial(local, mesh.shape["tgt"], mesh.shape["src"]),
        mesh=mesh,
        in_specs=placed,
        out_specs=P("tgt", None, "src", None),
        check_vma=False,
    )
```
